256 devices in a mesh: expert: 32 (over y, x, core), group: 8 (over z).
Axes of the slice: x: 4, y: 4, z: 8, core: 2. Of those that a mesh axis runs over, the one named last changes fastest.
Arguments:
- activations: bfloat16 [4096, 7168], P('expert', 'group'), may hold values from -6 to 6
- out_grads: bfloat16 [4096, 7168], P('expert', 'group'), may hold values from -6 to 6
- sketch_op: bfloat16 [7168, 128], P('group'), may hold values from -0.0625 to 0.0625
- block_lists: int32 [256, 32], P('expert'), may hold values from 0 to 31, as said below
- block_counts: int32 [256], P('expert'), may hold values from 1 to 32
- gate_values: bfloat16 [256, 32, 128], P('expert'), may hold values from 0.05 to 9, as said below
Outputs:
- basis_out: float32 [256, 7168, 128], P('expert', 'group')
The draws below stay inside these ranges and needn't reach their ends.
Inputs may be any that keep to these rules, and one draw needn't show every extreme that they name: `block_lists`: each row is an ordering of all 32 block numbers, each once. `gate_values`: positive.
All inputs are finite; a program needn't handle non-finite values.
Results may differ from the reference program's by a relative error of at most 0.0042.
The reference program's roundings to bfloat16 on the way (of `sketched` and `scaled`) count: a program that leaves them out, or rounds other values in their place, can miss the bound.
Values may be sent and summed in bfloat16 or wider, within the bound.
No kernel may reach another device: no remote copies, remote signals or barrier semaphores. Data moves between devices by JAX's collectives and lax.ppermute only.
A program may use at most 64 MiB of HBM per device.

```python
import math
import jax
import jax.numpy as jnp
from jax import lax

D = 7168
EXPERTS = 256
R = 128
BLK = 128
BLOCKS = 32
TOKENS = 4096


def draw_block_lists(key, part):
    sub_keys = jax.random.split(jax.random.fold_in(key, 11), EXPERTS)
    return jax.vmap(lambda sub_key: jax.random.permutation(sub_key, BLOCKS))(sub_keys).astype(jnp.int32)


def draw_block_counts(key, part):
    key_first, key_second, key_third = jax.random.split(jax.random.fold_in(key, 23), 3)
    first_draw = jax.random.randint(key_first, (EXPERTS,), 1, BLOCKS + 1)
    second_draw = jax.random.randint(key_second, (EXPERTS,), 1, BLOCKS + 1)
    counts = jnp.maximum(first_draw * second_draw // BLOCKS, 1)
    hot_expert = jax.random.randint(key_third, (), 0, EXPERTS)
    return jnp.where(jnp.arange(EXPERTS) == hot_expert, BLOCKS, counts).astype(jnp.int32)


def draw_gate_values(key, part):
    uniform_draw = jax.random.uniform(jax.random.fold_in(key, 37), (EXPERTS, BLOCKS, BLK), jnp.float32)
    ramp = jnp.arange(EXPERTS, dtype=jnp.float32) / (EXPERTS - 1)
    values = (0.1 + 0.9 * uniform_draw) * (1.0 + 2.0 * ramp)[:, None, None]
    return values.astype(jnp.bfloat16)


def block_levels(rng, shape, shards, smallest, top_value):
    loudness = 1.0
    for dim, blocks in shards:
        draws = jax.random.uniform(jax.random.fold_in(jax.random.fold_in(rng, 6), dim), (blocks,), jnp.float32, smallest / len(shards), top_value / len(shards))
        loudness = loudness * jnp.repeat(jnp.exp(draws), shape[dim] // blocks).reshape((-1,) + (1,) * (len(shape) - 1 - dim))
    return loudness


def centred(rng, shape, width, most, shards=(), kind=jnp.bfloat16):
    array = width * jax.random.normal(rng, shape, jnp.float32)
    if shards:
        array = array * block_levels(rng, shape, shards, -0.22, 0.18)
    return jnp.clip(array, -most, most).astype(kind)


def setup_inputs(seed: int = 0) -> dict:
    splits = jax.random.split(jax.random.key(seed), 7)
    return {
        "activations": centred(splits[0], (TOKENS, D), 1.0, 6.0, ((0, 32), (1, 8))),
        "out_grads": centred(splits[1], (TOKENS, D), 1.0, 6.0, ((0, 32), (1, 8))),
        "sketch_op": centred(splits[2], (D, R), D ** -0.5, 0.0625, ((0, 8),)),
        "block_lists": draw_block_lists(jax.random.fold_in(splits[6], 71), 0),
        "block_counts": draw_block_counts(jax.random.fold_in(splits[6], 71), 0),
        "gate_values": draw_gate_values(jax.random.fold_in(splits[6], 71), 0),
    }


def reference(activations, out_grads, sketch_op, block_lists, block_counts, gate_values):
    sketch_rank = sketch_op.shape[1]
    feat_width = activations.shape[1]
    sketched = jnp.dot(out_grads.astype(jnp.float32), sketch_op.astype(jnp.float32), preferred_element_type=jnp.float32).astype(jnp.bfloat16)
    act_blocks = activations.reshape(BLOCKS, BLK, feat_width)
    sketch_blocks = sketched.reshape(BLOCKS, BLK, sketch_rank)

    def expert_sketch(inputs):
        list_row, count_row, gate_block = inputs

        def add_block(slot, running):
            block_id = list_row[slot]
            rows_x = lax.dynamic_index_in_dim(act_blocks, block_id, 0, keepdims=False)
            rows_y = lax.dynamic_index_in_dim(sketch_blocks, block_id, 0, keepdims=False)
            gate_row = lax.dynamic_index_in_dim(gate_block, slot, 0, keepdims=False).astype(jnp.float32)
            scaled = (gate_row[:, None] * rows_y.astype(jnp.float32)).astype(jnp.bfloat16)
            return running + jnp.dot(rows_x.T.astype(jnp.float32), scaled.astype(jnp.float32), preferred_element_type=jnp.float32)
        return lax.fori_loop(0, count_row, add_block, jnp.zeros((feat_width, sketch_rank), jnp.float32))
    sketches = lax.map(expert_sketch, (block_lists, block_counts, gate_values))
    gram_total = jnp.einsum('edr,eds->rs', sketches, sketches, precision=lax.Precision.HIGHEST)
    factor = jnp.linalg.cholesky(gram_total)
    basis_flat = lax.linalg.triangular_solve(factor, sketches.reshape(-1, sketch_rank), left_side=False, lower=True, transpose_a=True)
    return (basis_flat * math.sqrt(EXPERTS * D)).reshape(EXPERTS, D, sketch_rank)
```

```python
import functools
import math

import jax
import jax.numpy as jnp
from jax import lax
from jax.experimental import pallas as pl
from jax.experimental.pallas import tpu as pltpu
from jax.sharding import PartitionSpec as P


F32 = jnp.float32
BF16 = jnp.bfloat16
SIDE = 4
DEPTH = 8
STEPS = (0, -1, 1, 2)


def place(y, x, core):
    return ((y % SIDE) * SIDE + x % SIDE) * 2 + core


def in_plane(value, move):
    pairs = [
        (place(y, x, core), place(*move(y, x, core)))
        for y in range(SIDE)
        for x in range(SIDE)
        for core in range(2)
    ]
    return lax.ppermute(value, "expert", pairs)


def swap_cores(value):
    return in_plane(value, lambda y, x, core: (y, x, 1 - core))


def first_axis(step):
    return lambda y, x, core: (y, x + step, core) if core == 0 else (y + step, x, core)


def second_axis(step):
    return lambda y, x, core: (y + step, x, core) if core == 0 else (y, x + step, core)


def ring_partner(x, stage):
    return x ^ 1 if stage == 0 else 3 - x


def along_x(stage):
    return lambda y, x, core: (y, ring_partner(x, stage ^ core), core)


def along_y(stage):
    return lambda y, x, core: (ring_partner(y, stage ^ core), x, core)


def depth_partner(z, stage):
    if stage == 0:
        return z ^ 1
    if stage == 1:
        return (z + 1) % DEPTH if z % 2 else (z - 1) % DEPTH
    return {0: 3, 3: 0, 1: 6, 6: 1, 2: 5, 5: 2, 4: 7, 7: 4}[z]


def along_z(value, stage):
    pairs = []
    for spot in range(SIDE * SIDE * 2):
        core = spot % 2
        for z in range(DEPTH):
            other = (depth_partner((z - core) % DEPTH, stage) + core) % DEPTH
            pairs.append((spot * DEPTH + z, spot * DEPTH + other))
    return lax.ppermute(value, ("expert", "group"), pairs)


def sum_over_depth(value):
    for stage in range(3):
        value = value + along_z(value, stage)
    return value


def split_kernel(core_ref, acts_ref, keep_ref, give_ref, turned_ref):
    half = keep_ref.shape[0]
    turned_ref[...] = acts_ref[...].T
    core = core_ref[0]
    keep_ref[...] = turned_ref[pl.ds(pl.multiple_of(core * half, 16), half), :]
    give_ref[...] = turned_ref[pl.ds(pl.multiple_of((1 - core) * half, 16), half), :]


def split_features(core, acts):
    tokens, width = acts.shape
    half = width // 2
    out = jax.ShapeDtypeStruct((half, tokens), acts.dtype)
    return pl.pallas_call(
        split_kernel,
        out_shape=(out, out),
        in_specs=[pl.BlockSpec(memory_space=pltpu.SMEM), pl.BlockSpec(memory_space=pltpu.VMEM)],
        out_specs=(pl.BlockSpec(memory_space=pltpu.VMEM),) * 2,
        scratch_shapes=[pltpu.VMEM((width, tokens), acts.dtype)],
        name="split_features",
    )(core, acts)


def product_kernel(row, first, last, experts, rank, *refs):
    ids_ref, acts_ref, sketch_ref, weight_ref = refs[:4]
    rest = list(refs[4:])
    prior_ref = None if first else rest.pop(0)
    total_ref = rest.pop(0)
    gram_ref = rest.pop(0) if last else None
    scaled_ref = rest.pop(0)
    chips, _, tokens = acts_ref.shape
    for i in range(chips):
        weight = weight_ref[ids_ref[row * chips + i]].astype(F32).T
        rows = sketch_ref[i].astype(F32)
        for e in range(experts):
            scaled_ref[i * tokens : (i + 1) * tokens, e * rank : (e + 1) * rank] = (
                weight[:, e : e + 1] * rows
            ).astype(BF16)
    gram = jnp.zeros((rank, 2 * rank), F32)
    acts = jnp.concatenate([acts_ref[i] for i in range(chips)], axis=1)
    for n in range(experts // 2):
        cols = slice(n * 2 * rank, (n + 1) * 2 * rank)
        part = jnp.dot(acts, scaled_ref[:, cols], preferred_element_type=F32)
        if not first:
            part = part + prior_ref[:, cols]
        total_ref[:, cols] = part
        if last:
            for k in range(2):
                piece = part[:, k * rank : (k + 1) * rank]
                high = piece.astype(BF16)
                low = (piece - high.astype(F32)).astype(BF16)
                gram = gram + lax.dot_general(
                    high,
                    jnp.concatenate([high, low], axis=1),
                    (((0,), (0,)), ((), ())),
                    preferred_element_type=F32,
                )
    if last:
        cross = gram[:, rank:]
        gram_ref[...] = gram[:, :rank] + (cross + cross.T)


def product(row, ids, acts, sketch, weight, prior, last):
    chips, half, tokens = acts.shape
    rank = sketch.shape[2]
    experts = weight.shape[1]
    first = prior is None
    total = jax.ShapeDtypeStruct((half, experts * rank), F32)
    vmem = pl.BlockSpec(memory_space=pltpu.VMEM)
    args = [ids, acts, sketch, weight] + ([] if first else [prior])
    return pl.pallas_call(
        functools.partial(product_kernel, row, first, last, experts, rank),
        out_shape=(total, jax.ShapeDtypeStruct((rank, rank), F32)) if last else total,
        in_specs=[pl.BlockSpec(memory_space=pltpu.SMEM)] + [vmem] * (len(args) - 1),
        out_specs=(vmem, vmem) if last else vmem,
        scratch_shapes=[pltpu.VMEM((chips * tokens, experts * rank), BF16)],
        input_output_aliases={} if first else {4: 0},
        compiler_params=pltpu.CompilerParams(vmem_limit_bytes=32 << 20),
        cost_estimate=pl.CostEstimate(
            flops=2 * half * chips * tokens * experts * rank,
            bytes_accessed=8 * half * experts * rank,
            transcendentals=0,
        ),
        name="product",
    )(*args)


def factor_kernel(scale, gram_ref, out_ref):
    size = gram_ref.shape[0]
    lanes = lax.broadcasted_iota(jnp.int32, (1, size), 1)
    work = gram_ref[...]
    rows = lax.broadcasted_iota(jnp.int32, (size, size), 0)
    cols = lax.broadcasted_iota(jnp.int32, (size, size), 1)
    unit = jnp.where(rows == cols, 1.0, 0.0).astype(F32)
    done = []
    group = 8
    pivots = jnp.zeros((1, size), F32)
    live_work, live_unit, base = work, unit, 0
    sub = lax.broadcasted_iota(jnp.int32, (size, 1), 0)
    for j in range(size):
        at = j - base
        column = live_work[:, j : j + 1]
        pivot_row = live_work[at : at + 1, :]
        unit_row = live_unit[at : at + 1, :]
        pivot = live_work[at : at + 1, j : j + 1]
        pivots = jnp.where(lanes == j, pivot, pivots)
        inverse = 1.0 / pivot
        factor = jnp.where(sub[base:, :] > j, column, 0.0)
        live_work = live_work - factor * (pivot_row * inverse)
        live_unit = live_unit - factor * (unit_row * inverse)
        if at == group - 1:
            done.append(live_unit[:group])
            live_work, live_unit, base = live_work[group:], live_unit[group:], base + group
    lower = jnp.concatenate(done, axis=0)
    out_ref[...] = lower.T * (scale * lax.rsqrt(pivots))


def inverse_factor(gram, scale):
    return pl.pallas_call(
        functools.partial(factor_kernel, scale),
        out_shape=jax.ShapeDtypeStruct(gram.shape, F32),
        in_specs=[pl.BlockSpec(memory_space=pltpu.VMEM)],
        out_specs=pl.BlockSpec(memory_space=pltpu.VMEM),
        name="inverse_factor",
    )(gram)


def basis_kernel(core_ref, mine_ref, theirs_ref, factor_ref, out_ref):
    half = mine_ref.shape[0]
    rank = factor_ref.shape[0]
    factor = factor_ref[...]
    high = factor.astype(BF16)
    low = (factor - high.astype(F32)).astype(BF16)
    right = jnp.concatenate(
        [
            jnp.concatenate([high, low], axis=1),
            jnp.concatenate([high, jnp.zeros_like(low)], axis=1),
        ],
        axis=0,
    )
    core = core_ref[0]
    for ref, spot in ((mine_ref, core), (theirs_ref, 1 - core)):
        piece = ref[...]
        top = piece.astype(BF16)
        rest = (piece - top.astype(F32)).astype(BF16)
        both = jnp.dot(jnp.concatenate([top, rest], axis=1), right, preferred_element_type=F32)
        out_ref[0, pl.ds(pl.multiple_of(spot * half, 8), half), :] = both[:, :rank] + both[:, rank:]


def basis(core, mine, theirs, factor, experts):
    half = mine.shape[0]
    rank = factor.shape[0]
    return pl.pallas_call(
        basis_kernel,
        grid=(experts,),
        out_shape=jax.ShapeDtypeStruct((experts, 2 * half, rank), F32),
        in_specs=[
            pl.BlockSpec(memory_space=pltpu.SMEM),
            pl.BlockSpec((half, rank), lambda e: (0, e)),
            pl.BlockSpec((half, rank), lambda e: (0, e)),
            pl.BlockSpec((rank, rank), lambda e: (0, 0)),
        ],
        out_specs=pl.BlockSpec((1, 2 * half, rank), lambda e: (e, 0, 0)),
        name="basis",
    )(core, mine, theirs, factor)


def on_device(activations, out_grads, sketch_op, block_lists, block_counts, gate_values):
    rank = sketch_op.shape[1]
    width = activations.shape[1]
    local_exp, blocks = block_lists.shape
    spot = lax.axis_index("expert").astype(jnp.int32)
    core = spot % 2
    here_x = (spot // 2) % SIDE
    here_y = spot // (2 * SIDE)
    core_arg = core.reshape(1)

    partial_sketch = jnp.dot(out_grads, sketch_op, preferred_element_type=F32)
    own_sketch = sum_over_depth(partial_sketch).astype(BF16)

    keep, give = split_features(core_arg, activations)
    got = swap_cores(give)
    unit = jnp.where(
        core == 0, jnp.concatenate([keep, got], axis=1), jnp.concatenate([got, keep], axis=1)
    )
    near = jnp.stack([unit] + [in_plane(unit, first_axis(-s)) for s in STEPS[1:]])
    far = [near] + [in_plane(near, second_axis(-s)) for s in STEPS[1:]]

    other_sketch = swap_cores(own_sketch)
    pair = jnp.where(
        core == 0,
        jnp.concatenate([own_sketch, other_sketch], axis=0),
        jnp.concatenate([other_sketch, own_sketch], axis=0),
    )
    near_sketch = jnp.stack([pair] + [in_plane(pair, first_axis(-s)) for s in STEPS[1:]])
    far_sketch = [near_sketch] + [in_plane(near_sketch, second_axis(-s)) for s in STEPS[1:]]

    slot_ids = jnp.arange(blocks, dtype=jnp.int32)
    slot_live = slot_ids[None, :] < block_counts[:, None]
    onehot = ((block_lists[:, :, None] == slot_ids[None, None, :]) & slot_live[:, :, None]).astype(
        BF16
    )
    weights = jnp.einsum("ejb,ejt->ebt", onehot, gate_values, preferred_element_type=F32).astype(
        BF16
    )
    weights = jnp.concatenate([weights, swap_cores(weights)], axis=0)
    weights = weights.reshape(2 * local_exp, blocks // 2, -1).transpose(1, 0, 2)

    ids = []
    for far_step in STEPS:
        for near_step in STEPS:
            step_x = jnp.where(core == 0, near_step, far_step)
            step_y = jnp.where(core == 0, far_step, near_step)
            ids.append(((here_y + step_y) % SIDE) * SIDE + (here_x + step_x) % SIDE)
    ids = jnp.stack(ids).astype(jnp.int32)

    total = None
    for row in range(SIDE):
        total = product(row, ids, far[row], far_sketch[row], weights, total, row == SIDE - 1)
    total, gram = total

    halves = gram.reshape(2, rank // 2, rank)
    keep_gram = lax.dynamic_index_in_dim(halves, core, 0, False)
    give_gram = lax.dynamic_index_in_dim(halves, 1 - core, 0, False)
    part = keep_gram + swap_cores(give_gram)
    theirs = swap_cores(total[:, local_exp * rank :])
    for move in (along_x(0), along_x(1), along_y(0), along_y(1)):
        part = part + in_plane(part, move)
    part = sum_over_depth(part)
    rest = swap_cores(part)
    gram_total = jnp.where(
        core == 0, jnp.concatenate([part, rest], axis=0), jnp.concatenate([rest, part], axis=0)
    )
    out_scale = math.sqrt(local_exp * lax.axis_size("expert") * width * lax.axis_size("group"))
    factor = inverse_factor(gram_total, out_scale)
    return basis(core_arg, total, theirs, factor, local_exp)


def solution(mesh):
    in_specs = (
        P("expert", "group"),
        P("expert", "group"),
        P("group", None),
        P("expert", None),
        P("expert"),
        P("expert", None, None),
    )
    out_specs = P("expert", "group", None)
    return jax.shard_map(
        on_device, mesh=mesh, in_specs=in_specs, out_specs=out_specs, check_vma=False
    )
```

```python
import functools
import math

import jax
import jax.numpy as jnp
from jax import lax
from jax.experimental import pallas as pl
from jax.experimental.pallas import tpu as pltpu
from jax.sharding import PartitionSpec as P


F32 = jnp.float32
BF16 = jnp.bfloat16
SIDE = 4
DEPTH = 8
STEPS = (0, -1, 1, 2)


def place(y, x, core):
    return ((y % SIDE) * SIDE + x % SIDE) * 2 + core


def in_plane(value, move):
    pairs = [
        (place(y, x, core), place(*move(y, x, core)))
        for y in range(SIDE)
        for x in range(SIDE)
        for core in range(2)
    ]
    return lax.ppermute(value, "expert", pairs)


def swap_cores(value):
    return in_plane(value, lambda y, x, core: (y, x, 1 - core))


def first_axis(step):
    return lambda y, x, core: (y, x + step, core) if core == 0 else (y + step, x, core)


def second_axis(step):
    return lambda y, x, core: (y + step, x, core) if core == 0 else (y, x + step, core)


def ring_partner(x, stage):
    return x ^ 1 if stage == 0 else 3 - x


def along_x(stage):
    return lambda y, x, core: (y, ring_partner(x, stage ^ core), core)


def along_y(stage):
    return lambda y, x, core: (ring_partner(y, stage ^ core), x, core)


def depth_partner(z, stage):
    if stage == 0:
        return z ^ 1
    if stage == 1:
        return (z + 1) % DEPTH if z % 2 else (z - 1) % DEPTH
    return {0: 3, 3: 0, 1: 6, 6: 1, 2: 5, 5: 2, 4: 7, 7: 4}[z]


def along_z(value, stage):
    pairs = []
    for spot in range(SIDE * SIDE * 2):
        core = spot % 2
        for z in range(DEPTH):
            other = (depth_partner((z - core) % DEPTH, stage) + core) % DEPTH
            pairs.append((spot * DEPTH + z, spot * DEPTH + other))
    return lax.ppermute(value, ("expert", "group"), pairs)


def sum_over_depth(value):
    for stage in range(3):
        value = value + along_z(value, stage)
    return value


def split_kernel(core_ref, mine_ref, theirs_ref, unit_ref, turned_ref):
    half = unit_ref.shape[0]
    tokens, width = mine_ref.shape
    span = turned_ref.shape[1]
    core = core_ref[0]
    for k, ref in enumerate((mine_ref, theirs_ref)):
        start = pl.multiple_of(core * (width - span), 128)
        turned_ref[k] = ref[:, pl.ds(start, span)].T
        inside = pl.multiple_of(core * (span - half), 16)
        unit_ref[:, k * tokens : (k + 1) * tokens] = turned_ref[k, pl.ds(inside, half), :]


def split_features(core, mine, theirs):
    tokens, width = mine.shape
    half = width // 2
    span = -(-half // 128) * 128
    vmem = pl.BlockSpec(memory_space=pltpu.VMEM)
    return pl.pallas_call(
        split_kernel,
        out_shape=jax.ShapeDtypeStruct((half, 2 * tokens), mine.dtype),
        in_specs=[pl.BlockSpec(memory_space=pltpu.SMEM), vmem, vmem],
        out_specs=vmem,
        scratch_shapes=[pltpu.VMEM((2, span, tokens), mine.dtype)],
        cost_estimate=pl.CostEstimate(flops=0, bytes_accessed=4 * tokens * width, transcendentals=0),
        name="split_features",
    )(core, mine, theirs)


def weigh_kernel(counts_ref, lists_ref, gates_ref, out_ref):
    experts, blocks, _ = gates_ref.shape
    block = lax.broadcasted_iota(jnp.int32, (blocks, blocks), 0)
    slot = lax.broadcasted_iota(jnp.int32, (blocks, blocks), 1)
    for e in range(experts):
        hit = (lists_ref[e : e + 1, :] == block) & (slot < counts_ref[e])
        onehot = jnp.where(hit, 1.0, 0.0).astype(BF16)
        out_ref[:, e, :] = jnp.dot(onehot, gates_ref[e], preferred_element_type=F32)


def weigh(counts, lists, gates):
    experts, blocks, tokens = gates.shape
    vmem = pl.BlockSpec(memory_space=pltpu.VMEM)
    return pl.pallas_call(
        weigh_kernel,
        out_shape=jax.ShapeDtypeStruct((blocks, experts, tokens), F32),
        in_specs=[pl.BlockSpec(memory_space=pltpu.SMEM), vmem, vmem],
        out_specs=vmem,
        cost_estimate=pl.CostEstimate(
            flops=2 * experts * blocks * blocks * tokens,
            bytes_accessed=8 * experts * blocks * tokens,
            transcendentals=0,
        ),
        name="weigh",
    )(counts, lists, gates)


def product_kernel(side, last, *refs):
    ids_ref, core_ref = refs[:2]
    acts_refs = refs[2:6]
    sketch_refs = refs[6:10]
    weight_refs = refs[10:12]
    rest = list(refs[12:])
    prior_refs = (rest.pop(0), rest.pop(0)) if last else None
    total_refs = (rest.pop(0), rest.pop(0))
    gram_ref = rest.pop(0) if last else None
    scaled_ref, column_ref = rest
    chips, tokens, rank = sketch_refs[0].shape
    experts = weight_refs[0].shape[1]
    pairs = experts // 2
    chunks = [(j, i) for j in range(SIDE) for i in range(SIDE)]
    block_side = core_ref[0] ^ side
    for k, (j, i) in enumerate(chunks):
        block = ids_ref[j * SIDE + i] * 2 + block_side
        weight = jnp.concatenate([weight_refs[0][block], weight_refs[1][block]], axis=0)
        column_ref[k * tokens : (k + 1) * tokens, : 2 * experts] = weight.T
    acts = jnp.concatenate(
        [acts_refs[j][i, :, side * tokens : (side + 1) * tokens] for j, i in chunks], axis=1
    )

    def fill(n):
        for k, (j, i) in enumerate(chunks):
            rows = sketch_refs[j][i] if side == 0 else sketch_refs[i][j]
            for h in range(2):
                e = 2 * n + h
                column = column_ref[k * tokens : (k + 1) * tokens, e : e + 1]
                scaled_ref[n % 2, k * tokens : (k + 1) * tokens, h * rank : (h + 1) * rank] = (
                    jnp.broadcast_to(column, (tokens, rank)).astype(BF16) * rows
                )

    gram = jnp.zeros((rank, 2 * rank), F32)
    fill(0)
    for n in range(experts):
        if n + 1 < experts:
            fill(n + 1)
        part = jnp.dot(acts, scaled_ref[n % 2], preferred_element_type=F32)
        owner, at = divmod(n, pairs)
        cols = slice(at * 2 * rank, (at + 1) * 2 * rank)
        if last:
            part = part + prior_refs[owner][:, cols]
        total_refs[owner][:, cols] = part
        if last:
            for k in range(2):
                piece = part[:, k * rank : (k + 1) * rank]
                high = piece.astype(BF16)
                low = (piece - high.astype(F32)).astype(BF16)
                gram = gram + lax.dot_general(
                    high,
                    jnp.concatenate([high, low], axis=1),
                    (((0,), (0,)), ((), ())),
                    preferred_element_type=F32,
                )
    if last:
        cross = gram[:, rank:]
        gram_ref[...] = gram[:, :rank] + (cross + cross.T)


def product(side, ids, core, acts, sketch, weights, prior):
    chips, half, unit = acts[0].shape
    tokens, rank = sketch[0].shape[1:]
    experts = weights[0].shape[1]
    last = prior is not None
    total = jax.ShapeDtypeStruct((half, experts * rank), F32)
    vmem = pl.BlockSpec(memory_space=pltpu.VMEM)
    smem = pl.BlockSpec(memory_space=pltpu.SMEM)
    args = [*acts, *sketch, *weights] + (list(prior) if last else [])
    outs = [total, total] + ([jax.ShapeDtypeStruct((rank, rank), F32)] if last else [])
    depth = SIDE * chips * tokens
    return pl.pallas_call(
        functools.partial(product_kernel, side, last),
        out_shape=tuple(outs),
        in_specs=[smem, smem] + [vmem] * len(args),
        out_specs=(vmem,) * len(outs),
        scratch_shapes=[
            pltpu.VMEM((2, depth, 2 * rank), BF16),
            pltpu.VMEM((depth, 128), F32),
        ],
        input_output_aliases={12: 0, 13: 1} if last else {},
        compiler_params=pltpu.CompilerParams(vmem_limit_bytes=32 << 20),
        cost_estimate=pl.CostEstimate(
            flops=4 * half * depth * experts * rank,
            bytes_accessed=16 * half * experts * rank,
            transcendentals=0,
        ),
        name="product",
    )(ids, core, *args)


def factor_kernel(scale, core_ref, part_ref, rest_ref, out_ref, gram_ref):
    share, size = part_ref.shape
    core = core_ref[0]
    gram_ref[pl.ds(pl.multiple_of(core * share, 8), share), :] = part_ref[...]
    gram_ref[pl.ds(pl.multiple_of((1 - core) * share, 8), share), :] = rest_ref[...]
    group = 8
    lanes = lax.broadcasted_iota(jnp.int32, (1, size), 1)
    rows = lax.broadcasted_iota(jnp.int32, (size, size), 0)
    cols = lax.broadcasted_iota(jnp.int32, (size, size), 1)
    left = gram_ref[...]
    right = jnp.where(rows == cols, 1.0, 0.0).astype(F32)
    inverses = jnp.zeros((1, size), F32)
    done = []
    for base in range(0, size, group):
        live = size - base
        sub = lax.broadcasted_iota(jnp.int32, (live, size), 0)
        column = [
            jnp.broadcast_to(left[:, base + k : base + k + 1], (live, size)) for k in range(group)
        ]
        lrow = [left[k : k + 1, :] for k in range(group)]
        rrow = [right[k : k + 1, :] for k in range(group)]
        for k in range(group):
            inverse = 1.0 / column[k][k : k + 1, :]
            inverses = jnp.where(lanes == base + k, inverse, inverses)
            lstep = lrow[k] * inverse
            rstep = rrow[k] * inverse
            for m in range(k + 1, group):
                down = column[k][m : m + 1, :]
                lrow[m] = lrow[m] - down * lstep
                rrow[m] = rrow[m] - down * rstep
                column[m] = column[m] - column[k] * (column[m][k : k + 1, :] * inverse)
            below = jnp.where(sub > k, column[k], 0.0)
            left = left - below * lstep
            right = right - below * rstep
        done.append(right[:group])
        left, right = left[group:], right[group:]
    lower = jnp.concatenate(done, axis=0)
    out_ref[...] = lower.T * (scale * jnp.sqrt(inverses))


def inverse_factor(core, part, rest, scale):
    size = part.shape[1]
    vmem = pl.BlockSpec(memory_space=pltpu.VMEM)
    return pl.pallas_call(
        functools.partial(factor_kernel, scale),
        out_shape=jax.ShapeDtypeStruct((size, size), F32),
        in_specs=[pl.BlockSpec(memory_space=pltpu.SMEM), vmem, vmem],
        out_specs=vmem,
        scratch_shapes=[pltpu.VMEM((size, size), F32)],
        name="inverse_factor",
    )(core, part, rest)


def halve_kernel(core_ref, mine_ref, theirs_ref, out_ref):
    experts, _, width = out_ref.shape
    half = mine_ref.shape[0]
    rank = width // 2
    core = core_ref[0]
    for ref, spot in ((mine_ref, core), (theirs_ref, 1 - core)):
        rows = pl.ds(pl.multiple_of(spot * half, 16), half)
        for e in range(experts):
            piece = ref[:, e * rank : (e + 1) * rank]
            high = piece.astype(BF16)
            out_ref[e, rows, :rank] = high
            out_ref[e, rows, rank:] = (piece - high.astype(F32)).astype(BF16)


def halve(core, mine, theirs, rank):
    half, flat = mine.shape
    experts = flat // rank
    vmem = pl.BlockSpec(memory_space=pltpu.VMEM)
    return pl.pallas_call(
        halve_kernel,
        out_shape=jax.ShapeDtypeStruct((experts, 2 * half, 2 * rank), BF16),
        in_specs=[pl.BlockSpec(memory_space=pltpu.SMEM), vmem, vmem],
        out_specs=vmem,
        cost_estimate=pl.CostEstimate(
            flops=4 * half * flat, bytes_accessed=16 * half * flat, transcendentals=0
        ),
        name="halve",
    )(core, mine, theirs)


def basis_kernel(halves_ref, factor_ref, out_ref):
    rank = factor_ref.shape[0]
    factor = factor_ref[...]
    high = factor.astype(BF16)
    low = (factor - high.astype(F32)).astype(BF16)
    right = jnp.concatenate(
        [
            jnp.concatenate([high, low], axis=1),
            jnp.concatenate([high, jnp.zeros_like(low)], axis=1),
        ],
        axis=0,
    )
    both = jnp.dot(halves_ref[0], right, preferred_element_type=F32)
    out_ref[0] = both[:, :rank] + both[:, rank:]


def basis(halves, factor):
    experts, width, _ = halves.shape
    rank = factor.shape[0]
    return pl.pallas_call(
        basis_kernel,
        grid=(experts,),
        out_shape=jax.ShapeDtypeStruct((experts, width, rank), F32),
        in_specs=[
            pl.BlockSpec((1, width, 2 * rank), lambda e: (e, 0, 0)),
            pl.BlockSpec((rank, rank), lambda e: (0, 0)),
        ],
        out_specs=pl.BlockSpec((1, width, rank), lambda e: (e, 0, 0)),
        name="basis",
    )(halves, factor)


def on_device(activations, out_grads, sketch_op, block_lists, block_counts, gate_values):
    rank = sketch_op.shape[1]
    width = activations.shape[1]
    local_exp, blocks = block_lists.shape
    spot = lax.axis_index("expert").astype(jnp.int32)
    core = spot % 2
    here_x = (spot // 2) % SIDE
    here_y = spot // (2 * SIDE)
    core_arg = core.reshape(1)
    hops = STEPS[1:]

    partial_sketch = jnp.dot(out_grads, sketch_op, preferred_element_type=F32)
    own_sketch = sum_over_depth(partial_sketch).astype(BF16)

    unit = split_features(core_arg, activations, swap_cores(activations))
    near = jnp.stack([unit] + [in_plane(unit, first_axis(-s)) for s in hops])
    acts = [near] + [in_plane(near, second_axis(-s)) for s in hops]

    near_own = jnp.stack([own_sketch] + [in_plane(own_sketch, first_axis(-s)) for s in hops])
    near_other = swap_cores(near_own)
    other = [near_other] + [in_plane(near_other, first_axis(-s)) for s in hops]
    own = [near_own] + [swap_cores(value) for value in other[1:]]

    weight = weigh(block_counts, block_lists, gate_values)
    weights = (weight, swap_cores(weight))

    ids = []
    for far_step in STEPS:
        for near_step in STEPS:
            step_x = jnp.where(core == 0, near_step, far_step)
            step_y = jnp.where(core == 0, far_step, near_step)
            ids.append(((here_y + step_y) % SIDE) * SIDE + (here_x + step_x) % SIDE)
    ids = jnp.stack(ids).astype(jnp.int32)

    total = product(1, ids, core_arg, acts, other, weights, None)
    mine, lent, gram = product(0, ids, core_arg, acts, own, weights, total)

    halves = gram.reshape(2, rank // 2, rank)
    keep_gram = lax.dynamic_index_in_dim(halves, core, 0, False)
    give_gram = lax.dynamic_index_in_dim(halves, 1 - core, 0, False)
    part = keep_gram + swap_cores(give_gram)
    theirs = swap_cores(lent)
    for move in (along_x(0), along_x(1), along_y(0), along_y(1)):
        part = part + in_plane(part, move)
    part = sum_over_depth(part)
    out_scale = math.sqrt(local_exp * lax.axis_size("expert") * width * lax.axis_size("group"))
    factor = inverse_factor(core_arg, part, swap_cores(part), out_scale)
    return basis(halve(core_arg, mine, theirs, rank), factor)


def solution(mesh):
    in_specs = (
        P("expert", "group"),
        P("expert", "group"),
        P("group", None),
        P("expert", None),
        P("expert"),
        P("expert", None, None),
    )
    out_specs = P("expert", "group", None)
    return jax.shard_map(
        on_device, mesh=mesh, in_specs=in_specs, out_specs=out_specs, check_vma=False
    )
```
